32 devices in a mesh: cfg: 2 (over x), work: 16 (over z, y, core).
Axes of the slice: x: 2, y: 2, z: 4, core: 2. Of those that a mesh axis runs over, the one named last changes fastest.
Arguments:
- sources: bfloat16 [32, 16384, 128], P('cfg', 'work'), parts along dimension 0, may hold values from -6 to 6
- perambs: bfloat16 [192, 16384], P('cfg', 'work'), parts along dimension 0, may hold values from -0.5 to 0.5
- source_ids: int32 [16], replicated, may hold values from 0 to 15
- peramb_ids: int32 [48, 3], replicated, may hold values from 0 to 95
- sink_counts: int32 [16], replicated, may hold values from 1 to 6, 48 in all
- weights: float32 [48], replicated, may hold values from -2 to 2, as said below
Outputs:
- sink_tensors: bfloat16 [32, 16384, 128], P(('cfg', 'work')), parts along dimension 0
The draws below stay inside these ranges and needn't reach their ends.
There are 2 independent parts, one for each index of `cfg`. The reference program is written for one: setup_inputs(seed, part) draws one part's arguments, and reference() takes and returns one part's arrays. A program takes and returns all parts, laid end to end along the dimension named above; an argument that names none is the same for every part. Nothing has to cross between parts.
Inputs may be any that keep to these rules, and one draw needn't show every extreme that they name: `sink_counts`: diagrams are listed sink by sink in order; the counts add up to 48 and some sink has exactly 6 diagrams. `weights`: nonzero multiples of 1/4.
All inputs are finite; a program needn't handle non-finite values.
Results may differ from the reference program's by a relative error of at most 0.0064.
Values may be sent and summed in bfloat16 or wider, within the bound.
A program may use at most 128 MiB of HBM per device.

```python
import math
import jax
import jax.numpy as jnp
import numpy as np
from jax import lax

N = 128
MOST = 6
SRC = 16
PERAMB = 96
DIAG = 48
SINK = 16


def draw_weights(key, part):
    key_mag, key_sign = jax.random.split(key)
    magnitude = jax.random.randint(key_mag, (DIAG,), 1, 9).astype(jnp.float32)
    signs = 2.0 * jax.random.randint(key_sign, (DIAG,), 0, 2).astype(jnp.float32) - 1.0
    return magnitude * signs * 0.25


def set_ends(drawn, rng, smallest, top_value):
    shape = drawn.shape
    place = [jax.random.randint(jax.random.fold_in(rng, axis), (), 0, shape[axis]) for axis in range(len(shape))]
    drawn = drawn.at[tuple(place)].set(smallest)
    longest = shape.index(max(shape))
    place[longest] = (place[longest] + 1) % shape[longest]
    return drawn.at[tuple(place)].set(top_value)


def steps_of(stream_key, shape, pieces, low, high):
    def one(position, blocks):
        heights = jax.random.uniform(jax.random.fold_in(jax.random.fold_in(stream_key, 6), position), (blocks,), jnp.float32, low / len(pieces), high / len(pieces))
        return jnp.repeat(jnp.exp(heights), shape[position] // blocks).reshape((-1,) + (1,) * (len(shape) - position - 1))

    level = one(*pieces[0])
    for cut in pieces[1:]:
        level = level * one(*cut)
    return level


def cumulative_ranks(number_of, slope):
    weights = [(1 << 20) // math.isqrt(standing ** slope) + 1 for standing in range(1, number_of + 1)]
    spread = 1 + sum(weights) // (1 << 30)
    return np.cumsum(np.array([max(1, weight // spread) for weight in weights]))


def skewed_ids(own_key, shape, number_of, lean):
    table = cumulative_ranks(number_of, lean)
    lot = jax.random.randint(jax.random.fold_in(own_key, 1), shape, 0, int(table[number_of - 1]))
    standing = jnp.searchsorted(jnp.asarray(table, jnp.int32), lot, side="right")
    return jax.random.permutation(jax.random.fold_in(own_key, 2), number_of)[standing].astype(jnp.int32)


def split_up(count, total, limit, lean):
    weights = [(1 << 20) // math.isqrt(standing ** lean) + 1 for standing in range(2, count + 1)]
    surplus, holding = total - limit - (count - 1), [1] * (count - 1)
    while surplus > 0:
        free = [i for i in range(count - 1) if holding[i] < limit]
        mass, left = sum([weights[i] for i in free]), surplus
        for i in free:
            extra = min(limit - holding[i], max(1, left * weights[i] // mass), surplus)
            holding[i] = holding[i] + extra
            surplus = surplus - extra
    return np.array([limit] + holding)


def uneven(own_key, count, total, bound, lean):
    if count == 2:
        one = jax.random.randint(own_key, (), max(1, total - bound), min(bound, total - 1) + 1)
        return jnp.stack([one, total - one])
    lengths = jnp.asarray(split_up(count, total, bound, lean), jnp.int32)
    twos = (count - 1) // 2
    source_of, sink = lengths[1:1 + 2 * twos:2], lengths[2:2 + 2 * twos:2]
    margin = jnp.minimum(source_of - 1, bound - sink)
    moved = jax.random.randint(jax.random.fold_in(own_key, 1), (twos,), 0, 1 << 20) % (margin + 1)
    lengths = lengths.at[1:1 + 2 * twos:2].set(source_of - moved).at[2:2 + 2 * twos:2].set(sink + moved)
    return lengths[jax.random.permutation(jax.random.fold_in(own_key, 2), count)]


def normal_values(rng, dims, deviation, bound, cuts=(), kind=jnp.bfloat16):
    drawn = jax.random.normal(rng, dims, jnp.float32) * deviation
    if len(cuts) > 0:
        drawn = steps_of(rng, dims, cuts, -0.22, 0.18) * drawn
    return jnp.clip(drawn, min=-bound, max=bound).astype(kind)


def setup_inputs(seed: int = 0, part: int = 0) -> dict:
    keys = jax.random.split(jax.random.key(seed), 7)
    part_splits = jax.random.split(jax.random.fold_in(keys[6], part), 7)
    return {
        "sources": normal_values(part_splits[0], (SRC, N * N, N), 1.0, 6.0, ((1, 16),)),
        "perambs": normal_values(part_splits[1], (PERAMB, N * N), N ** -0.5, 0.5, ((1, 16),)),
        "source_ids": set_ends(skewed_ids(keys[2], (SINK,), SRC, 2), jax.random.fold_in(keys[2], 3), 0, SRC - 1).astype(jnp.int32),
        "peramb_ids": set_ends(jax.random.randint(keys[3], (DIAG, 3), 0, PERAMB), jax.random.fold_in(keys[3], 1), 0, PERAMB - 1).astype(jnp.int32),
        "sink_counts": uneven(keys[4], SINK, DIAG, MOST, 2).astype(jnp.int32),
        "weights": draw_weights(jax.random.fold_in(keys[6], 71), part),
    }


def contract(tensor_rows, leg_mats):
    extent = tensor_rows.shape[1]
    third = jnp.dot(tensor_rows, leg_mats[2].T, preferred_element_type=jnp.float32).astype(jnp.bfloat16)
    third = third.reshape(extent, extent, extent)
    second = jnp.einsum("bk,akc->abc", leg_mats[1].astype(jnp.float32), third.astype(jnp.float32)).astype(jnp.bfloat16)
    whole = jnp.dot(leg_mats[0], second.reshape(extent, extent * extent), preferred_element_type=jnp.float32)
    return whole.reshape(extent * extent, extent)


def reference(sources, perambs, source_ids, peramb_ids, sink_counts, weights):
    matrices = perambs.reshape(PERAMB, N, N)
    sink_ends = jnp.cumsum(sink_counts)
    sink_of = jnp.sum((sink_ends[None, :] <= jnp.arange(DIAG, dtype=jnp.int32)[:, None]).astype(jnp.int32), axis=1)

    def advance(totals, diagram):
        target = sink_of[diagram]
        tensor_rows = sources[source_ids[target]]
        leg_mats = matrices[peramb_ids[diagram]]
        weighted = (weights[diagram] * contract(tensor_rows, leg_mats)).astype(jnp.bfloat16)
        weighted = lax.optimization_barrier(weighted).astype(jnp.float32)
        current = lax.dynamic_index_in_dim(totals, target, 0, keepdims=False)
        totals = lax.dynamic_update_index_in_dim(totals, current + weighted, target, 0)
        return totals, None

    totals, unused = lax.scan(advance, jnp.zeros((SINK, N * N, N), jnp.float32), jnp.arange(DIAG, dtype=jnp.int32))
    return totals.astype(jnp.bfloat16)
```

```python
import functools

import jax
import jax.numpy as jnp
from jax import lax
from jax.experimental import pallas as pl
from jax.experimental.pallas import tpu as pltpu
from jax.sharding import PartitionSpec as P

MOST = 6
CHUNKS = 4


def copy_kernel(ids_ref, x_ref, o_ref):
    o_ref[...] = x_ref[...]


def pick_rows(sources, source_ids, part, parts):
    sinks = source_ids.shape[0]
    rows = sources.shape[1] // parts
    extent = sources.shape[2]
    return pl.pallas_call(
        copy_kernel,
        out_shape=jax.ShapeDtypeStruct((sinks, rows, extent), sources.dtype),
        grid_spec=pltpu.PrefetchScalarGridSpec(
            num_scalar_prefetch=1,
            grid=(sinks,),
            in_specs=[pl.BlockSpec((1, rows, extent), lambda s, ids: (ids[s], part, 0))],
            out_specs=pl.BlockSpec((1, rows, extent), lambda s, ids: (s, 0, 0)),
        ),
        cost_estimate=pl.CostEstimate(
            flops=0, transcendentals=0, bytes_accessed=4 * sinks * rows * extent
        ),
        name="pick_rows",
    )(source_ids, sources)


def contract_kernel(first, last, count, extent, w_ref, x_ref, p1_ref, p2_ref, p3_ref, *rest):
    if first:
        o_ref, mid = rest[0], rest[1]
        acc_in = None
    else:
        acc_in, o_ref, mid = rest[0], rest[1], rest[2]
    acc = rest[-1] if last else o_ref

    @pl.loop(0, count // 2)
    def _(pair):
        x0 = x_ref[2 * pair]
        x1 = x_ref[2 * pair + 1]
        both = jnp.concatenate([x0, x1], axis=1)
        z = jnp.dot(p2_ref[...], both, preferred_element_type=jnp.float32).astype(jnp.bfloat16)
        for d in range(MOST):
            zd = z[d * extent : (d + 1) * extent]
            stacked = jnp.concatenate([zd[:, :extent], zd[:, extent:]], axis=0)
            y = jnp.dot(stacked, p3_ref[d], preferred_element_type=jnp.float32) * w_ref[d]
            mid[pl.ds(pl.multiple_of((d * count + 2 * pair) * extent, extent), 2 * extent), :] = y

    @pl.loop(0, extent // 2)
    def _(b):
        cols = []
        for h in range(2):
            cols.append(
                mid[pl.ds(2 * b + h, MOST * count, stride=extent), :].astype(jnp.bfloat16)
            )
        rhs = jnp.concatenate(cols, axis=1)
        t = jnp.dot(p1_ref[...], rhs, preferred_element_type=jnp.float32)
        for h in range(2):
            at = pl.ds(pl.multiple_of((2 * b + h) * extent, extent), extent)
            part = t[:, h * extent : (h + 1) * extent]
            if not first:
                part = part + acc_in[at, :]
            acc[at, :] = part

    if last:

        @pl.loop(0, extent)
        def _(a):
            at = pl.ds(pl.multiple_of(a * extent, extent), extent)
            o_ref[at, :] = acc[pl.ds(a, extent, stride=extent), :].astype(jnp.bfloat16)


def contract(x, p1, p2, p3, w, total, last):
    count, extent = x.shape[0], x.shape[1]
    first = total is None
    vmem = pl.BlockSpec(memory_space=pltpu.VMEM)
    operands = [w, x, p1, p2, p3] + ([] if first else [total])
    scratch = [pltpu.VMEM((MOST * count * extent, extent), jnp.float32)]
    if last:
        scratch.append(pltpu.VMEM((extent * extent, extent), jnp.float32))
    return pl.pallas_call(
        functools.partial(contract_kernel, first, last, count, extent),
        out_shape=jax.ShapeDtypeStruct(
            (extent * extent, extent), jnp.bfloat16 if last else jnp.float32
        ),
        in_specs=[pl.BlockSpec(memory_space=pltpu.SMEM)] + [vmem] * (len(operands) - 1),
        out_specs=vmem,
        scratch_shapes=scratch,
        compiler_params=pltpu.CompilerParams(vmem_limit_bytes=60 * 1024 * 1024),
        cost_estimate=pl.CostEstimate(
            flops=6 * MOST * count * extent**3, transcendentals=0, bytes_accessed=16 * extent**3
        ),
        name="contract",
    )(*operands)


def per_device(sources, perambs, source_ids, peramb_ids, sink_counts, weights):
    workers = lax.axis_size("work")
    extent = sources.shape[2]
    own_a = sources.shape[1] // extent
    diagrams = peramb_ids.shape[0]
    parts = min(CHUNKS, own_a)
    per = own_a // parts

    moved = []
    for i in range(parts):
        picked = pick_rows(sources, source_ids, i, parts)
        moved.append(lax.all_to_all(picked, "work", split_axis=0, concat_axis=0, tiled=True))

    starts = jnp.cumsum(sink_counts) - sink_counts
    slots = jnp.arange(MOST, dtype=jnp.int32)
    chosen = jnp.minimum(starts[:, None] + slots[None, :], diagrams - 1)
    ids = peramb_ids[chosen].reshape(-1)
    onehot = (ids[:, None] == jnp.arange(perambs.shape[0], dtype=jnp.int32)[None, :]).astype(
        jnp.bfloat16
    )
    legs_send = jnp.dot(onehot, perambs, preferred_element_type=jnp.bfloat16)
    legs = lax.all_to_all(
        legs_send.reshape(workers, MOST * 3, -1), "work", split_axis=0, concat_axis=0, tiled=True
    )
    legs = (
        legs.reshape(workers, MOST, 3, -1, extent)
        .transpose(2, 1, 0, 3, 4)
        .reshape(3, MOST, extent, extent)
    )
    own = lax.axis_index("work")
    own_ids = lax.dynamic_index_in_dim(chosen, own, 0, keepdims=False)
    own_count = lax.dynamic_index_in_dim(sink_counts, own, 0, keepdims=False)
    w = jnp.where(slots < own_count, weights[own_ids], 0.0)
    p2 = legs[1].reshape(MOST * extent, extent)
    p3 = legs[2].transpose(0, 2, 1)
    p1 = (
        legs[0]
        .reshape(MOST, extent, workers, parts, per)
        .transpose(3, 1, 0, 2, 4)
        .reshape(parts, extent, MOST * workers * per)
    )
    total = None
    for i in range(parts):
        x = moved[i].reshape(workers * per, extent, extent)
        total = contract(x, p1[i], p2, p3, w, total, i == parts - 1)
    return total[None]


def solution(mesh):
    return jax.shard_map(
        per_device,
        mesh=mesh,
        in_specs=(P("cfg", "work", None), P("cfg", "work"), P(), P(), P(), P()),
        out_specs=P(("cfg", "work"), None, None),
        check_vma=False,
    )
```

```python
import functools

import jax
import jax.numpy as jnp
import numpy as np
from jax import lax
from jax.experimental import pallas as pl
from jax.experimental.pallas import tpu as pltpu
from jax.sharding import PartitionSpec as P

MOST = 6
LEGS = 3
CHUNKS = 4
PAD = 8
MESH = pl.DeviceIdType.MESH


def pick_kernel(ids_ref, x_ref, o_ref, buf, in_sem, out_sem):
    sinks = o_ref.shape[0]
    load = pltpu.make_async_copy(x_ref, buf, in_sem)
    load.start()
    load.wait()

    @pl.loop(0, sinks)
    def _(s):
        pltpu.make_async_copy(buf.at[ids_ref[s]], o_ref.at[s], out_sem.at[s]).start()

    @pl.loop(0, sinks)
    def _(s):
        pltpu.make_async_copy(buf.at[0], o_ref.at[s], out_sem.at[s]).wait()


def pick(sources, source_ids):
    sinks = source_ids.shape[0]
    shape = (sinks,) + sources.shape[1:]
    return pl.pallas_call(
        pick_kernel,
        out_shape=jax.ShapeDtypeStruct(shape, sources.dtype),
        in_specs=[
            pl.BlockSpec(memory_space=pltpu.SMEM),
            pl.BlockSpec(memory_space=pl.ANY),
        ],
        out_specs=pl.BlockSpec(memory_space=pl.ANY),
        scratch_shapes=[
            pltpu.VMEM(sources.shape, sources.dtype),
            pltpu.SemaphoreType.DMA,
            pltpu.SemaphoreType.DMA((sinks,)),
        ],
        compiler_params=pltpu.CompilerParams(vmem_limit_bytes=60 * 1024 * 1024),
        name="pick",
    )(source_ids, sources)


def contract_kernel(
    workers,
    parts,
    w_ref,
    key_ref,
    x_ref,
    legs_ref,
    o_ref,
    xbuf,
    lbuf,
    legs,
    p1s,
    p2s,
    p3s,
    mid,
    acc,
    obuf,
    own_sem,
    xsend,
    xrecv,
    lsend,
    lrecv,
    out_sem,
):
    per, extent = xbuf.shape[2], xbuf.shape[3]
    own_rows = lbuf.shape[2]
    count = workers * per
    step = extent + PAD
    me = lax.axis_index("work")

    def leg_copy(t):
        peer = lax.rem(me + t, workers)
        return pltpu.make_async_remote_copy(
            src_ref=legs_ref.at[peer],
            dst_ref=lbuf.at[me],
            send_sem=lsend.at[t],
            recv_sem=lrecv.at[t],
            device_id={"work": peer},
            device_id_type=MESH,
        )

    def x_copy(c, t):
        peer = lax.rem(me + t, workers)
        return pltpu.make_async_remote_copy(
            src_ref=x_ref.at[peer, pl.ds(c * per, per)],
            dst_ref=xbuf.at[c, me],
            send_sem=xsend.at[c, t],
            recv_sem=xrecv.at[c, t],
            device_id={"work": peer},
            device_id_type=MESH,
        )

    own = [pltpu.make_async_copy(legs_ref.at[me], lbuf.at[me], own_sem.at[parts])]
    for c in range(parts):
        own.append(
            pltpu.make_async_copy(
                x_ref.at[me, pl.ds(c * per, per)], xbuf.at[c, me], own_sem.at[c]
            )
        )
    for copy in own:
        copy.start()

    barrier = pltpu.get_barrier_semaphore()

    @pl.loop(1, workers)
    def _(t):
        peer = lax.rem(me + t, workers)
        pl.semaphore_signal(barrier, inc=1, device_id={"work": peer}, device_id_type=MESH)

    pl.semaphore_wait(barrier, workers - 1)

    @pl.loop(1, workers)
    def _(t):
        leg_copy(t).start()

    for c in range(parts):

        @pl.loop(1, workers)
        def _(t):
            x_copy(c, t).start()

    own[0].wait()

    @pl.loop(1, workers)
    def _(t):
        leg_copy(t).wait()

    @pl.loop(0, MOST * LEGS)
    def _(m):
        for v in range(workers):
            legs[m, v * own_rows : (v + 1) * own_rows, :] = lbuf[v, m].astype(jnp.float32)

    firsts = []
    for d in range(MOST):
        firsts.append(legs[LEGS * d].astype(jnp.bfloat16))
        p2s[d * extent : (d + 1) * extent, :] = legs[LEGS * d + 1].astype(jnp.bfloat16)
        p3s[d] = legs[LEGS * d + 2].T.astype(jnp.bfloat16)
    side = jnp.concatenate(firsts, axis=1)
    rows = lax.broadcasted_iota(jnp.int32, (MOST * extent, MOST * count), 0)
    for c in range(parts):
        chosen = jnp.where(rows == key_ref[c], 1.0, 0.0).astype(jnp.bfloat16)
        p1s[c] = jnp.dot(side, chosen, preferred_element_type=jnp.float32).astype(jnp.bfloat16)

    group = 4
    wide = 8
    for c in range(parts):
        own[c + 1].wait()

        @pl.loop(1, workers)
        def _(t):
            x_copy(c, t).wait()

        @pl.loop(0, count // group, unroll=2)
        def _(g):
            tiles = [xbuf[c, g * (group // per) + i // per, i % per] for i in range(group)]
            both = jnp.concatenate(tiles, axis=1)
            for d in range(MOST):
                z = jnp.dot(
                    p2s[d * extent : (d + 1) * extent, :], both, preferred_element_type=jnp.float32
                ).astype(jnp.bfloat16)
                stacked = jnp.concatenate(
                    [z[:, i * extent : (i + 1) * extent] for i in range(group)], axis=0
                )
                y = jnp.dot(stacked, p3s[d], preferred_element_type=jnp.float32) * w_ref[d]
                for i in range(group):
                    at = pl.multiple_of((d * count + group * g + i) * step, 8)
                    mid[pl.ds(at, extent), :] = y[i * extent : (i + 1) * extent]

        @pl.loop(0, extent // wide)
        def _(b):
            cols = [
                mid[pl.ds(wide * b + h, MOST * count, stride=step), :].astype(jnp.bfloat16)
                for h in range(wide)
            ]
            t = jnp.dot(
                p1s[c], jnp.concatenate(cols, axis=1), preferred_element_type=jnp.float32
            )
            for h in range(wide):
                at = pl.ds(pl.multiple_of((wide * b + h) * step, 8), extent)
                piece = t[:, h * extent : (h + 1) * extent]
                if c > 0:
                    piece = piece + acc[at, :]
                acc[at, :] = piece

    span = 16
    for g in range(extent // span):

        @pl.loop(0, span, unroll=4)
        def _(i):
            a = g * span + i
            obuf[a] = acc[pl.ds(a, extent, stride=step), :].astype(jnp.bfloat16)

        pltpu.make_async_copy(
            obuf.at[pl.ds(g * span, span)], o_ref.at[pl.ds(g * span, span)], out_sem.at[g]
        ).start()
    for g in range(extent // span):
        pltpu.make_async_copy(
            obuf.at[pl.ds(g * span, span)], o_ref.at[pl.ds(g * span, span)], out_sem.at[g]
        ).wait()


def contract(x, legs, w, workers):
    own_a, extent = x.shape[1], x.shape[2]
    parts = min(CHUNKS, own_a)
    per = own_a // parts
    count = workers * per
    col = np.arange(MOST * count)
    keys = [
        col // count * extent + col % count // per * own_a + c * per + col % per
        for c in range(parts)
    ]
    key = jnp.asarray(np.stack(keys)[:, None, :], jnp.int32)
    step = extent + PAD
    return pl.pallas_call(
        functools.partial(contract_kernel, workers, parts),
        out_shape=jax.ShapeDtypeStruct((extent, extent, extent), jnp.bfloat16),
        in_specs=[
            pl.BlockSpec(memory_space=pltpu.SMEM),
            pl.BlockSpec(memory_space=pltpu.VMEM),
            pl.BlockSpec(memory_space=pl.ANY),
            pl.BlockSpec(memory_space=pl.ANY),
        ],
        out_specs=pl.BlockSpec(memory_space=pl.ANY),
        scratch_shapes=[
            pltpu.VMEM((parts, workers, per, extent, extent), jnp.bfloat16),
            pltpu.VMEM((workers,) + legs.shape[1:], jnp.bfloat16),
            pltpu.VMEM((MOST * LEGS, extent, extent), jnp.float32),
            pltpu.VMEM((parts, extent, MOST * count), jnp.bfloat16),
            pltpu.VMEM((MOST * extent, extent), jnp.bfloat16),
            pltpu.VMEM((MOST, extent, extent), jnp.bfloat16),
            pltpu.VMEM((MOST * count * step, extent), jnp.float32),
            pltpu.VMEM((extent * step, extent), jnp.float32),
            pltpu.VMEM((extent, extent, extent), jnp.bfloat16),
            pltpu.SemaphoreType.DMA((parts + 1,)),
            pltpu.SemaphoreType.DMA((parts, workers)),
            pltpu.SemaphoreType.DMA((parts, workers)),
            pltpu.SemaphoreType.DMA((workers,)),
            pltpu.SemaphoreType.DMA((workers,)),
            pltpu.SemaphoreType.DMA((extent // 16,)),
        ],
        compiler_params=pltpu.CompilerParams(
            vmem_limit_bytes=62 * 1024 * 1024, collective_id=0, has_side_effects=True
        ),
        name="contract",
    )(w, key, x, legs)


def per_device(sources, perambs, source_ids, peramb_ids, sink_counts, weights):
    workers = lax.axis_size("work")
    extent = sources.shape[2]
    own_a = sources.shape[1] // extent
    diagrams = peramb_ids.shape[0]

    picked = pick(sources.reshape(-1, own_a, extent, extent), source_ids)
    starts = jnp.cumsum(sink_counts) - sink_counts
    slots = jnp.arange(MOST, dtype=jnp.int32)
    chosen = jnp.minimum(starts[:, None] + slots[None, :], diagrams - 1)
    ids = peramb_ids[chosen].reshape(-1)
    onehot = (ids[:, None] == jnp.arange(perambs.shape[0], dtype=jnp.int32)[None, :]).astype(
        jnp.bfloat16
    )
    legs = jnp.dot(onehot, perambs, preferred_element_type=jnp.bfloat16)
    legs = legs.reshape(workers, MOST * LEGS, -1, extent)
    own = lax.axis_index("work")
    own_ids = lax.dynamic_index_in_dim(chosen, own, 0, keepdims=False)
    own_count = lax.dynamic_index_in_dim(sink_counts, own, 0, keepdims=False)
    w = jnp.where(slots < own_count, weights[own_ids], 0.0)
    total = contract(picked, legs, w, workers)
    return total.reshape(1, extent * extent, extent)


def solution(mesh):
    return jax.shard_map(
        per_device,
        mesh=mesh,
        in_specs=(P("cfg", "work", None), P("cfg", "work"), P(), P(), P(), P()),
        out_specs=P(("cfg", "work"), None, None),
        check_vma=False,
    )
```

```python
import functools

import jax
import jax.numpy as jnp
import numpy as np
from jax import lax
from jax.experimental import pallas as pl
from jax.experimental.pallas import tpu as pltpu
from jax.sharding import PartitionSpec as P

MOST = 6
LEGS = 3
PAD = 8
MESH = pl.DeviceIdType.MESH


def pick_kernel(
    ids_ref, legs_ids_ref, counts_ref, x_ref, p_ref, o_ref, l_ref, buf, rows, in_sem, out_sem
):
    sinks = o_ref.shape[0]
    diagrams = legs_ids_ref.shape[0] // LEGS
    own_rows, extent = l_ref.shape[2], l_ref.shape[3]
    load = pltpu.make_async_copy(x_ref, buf, in_sem)
    load.start()

    for r in range(own_rows):
        rows[:, r, :] = p_ref[:, r * extent : (r + 1) * extent].astype(jnp.float32)

    load.wait()

    @pl.loop(0, sinks)
    def _(s):
        pltpu.make_async_copy(buf.at[ids_ref[s]], o_ref.at[s], out_sem.at[s]).start()

    def one(s, start):
        for slot in range(MOST):
            d = jnp.minimum(start + slot, diagrams - 1)
            for leg in range(LEGS):
                l_ref[s, slot * LEGS + leg] = rows[legs_ids_ref[d * LEGS + leg]].astype(
                    jnp.bfloat16
                )
        return start + counts_ref[s]

    lax.fori_loop(0, sinks, one, jnp.int32(0))

    @pl.loop(0, sinks)
    def _(s):
        pltpu.make_async_copy(buf.at[0], o_ref.at[s], out_sem.at[s]).wait()


def pick(sources, perambs, source_ids, leg_ids, counts):
    sinks = source_ids.shape[0]
    own_rows, extent = sources.shape[1], sources.shape[3]
    smem = pl.BlockSpec(memory_space=pltpu.SMEM)
    return pl.pallas_call(
        pick_kernel,
        out_shape=(
            jax.ShapeDtypeStruct((sinks,) + sources.shape[1:], sources.dtype),
            jax.ShapeDtypeStruct((sinks, MOST * LEGS, own_rows, extent), perambs.dtype),
        ),
        in_specs=[
            smem,
            smem,
            smem,
            pl.BlockSpec(memory_space=pl.ANY),
            pl.BlockSpec(memory_space=pltpu.VMEM),
        ],
        out_specs=(
            pl.BlockSpec(memory_space=pl.ANY),
            pl.BlockSpec(memory_space=pltpu.VMEM),
        ),
        scratch_shapes=[
            pltpu.VMEM(sources.shape, sources.dtype),
            pltpu.VMEM((perambs.shape[0], own_rows, extent), jnp.float32),
            pltpu.SemaphoreType.DMA,
            pltpu.SemaphoreType.DMA((sinks,)),
        ],
        compiler_params=pltpu.CompilerParams(vmem_limit_bytes=60 * 1024 * 1024),
        name="pick",
    )(source_ids, leg_ids, counts, sources, perambs)


def split_rows(own_a):
    sizes, left = [], own_a
    while left > 0:
        sizes.append(2 if left > 2 else 1)
        left -= sizes[-1]
    return sizes


def contract_kernel(
    workers,
    counts_ref,
    weights_ref,
    key_ref,
    x_ref,
    legs_ref,
    o_ref,
    xbuf,
    lbuf,
    legs,
    p1s,
    p2s,
    p3s,
    mid,
    acc,
    stage,
    obuf,
    own_sem,
    xsend,
    xrecv,
    lsend,
    lrecv,
    out_sem,
):
    own_a, extent = xbuf.shape[0], xbuf.shape[2]
    diagrams = weights_ref.shape[0]
    sizes = split_rows(own_a)
    step = extent + PAD
    me = lax.axis_index("work")

    def leg_copy(t):
        peer = lax.rem(me + t, workers)
        return pltpu.make_async_remote_copy(
            src_ref=legs_ref.at[peer],
            dst_ref=lbuf.at[me],
            send_sem=lsend.at[t],
            recv_sem=lrecv.at[t],
            device_id={"work": peer},
            device_id_type=MESH,
        )

    def x_copy(j, t):
        peer = lax.rem(me + t, workers)
        return pltpu.make_async_remote_copy(
            src_ref=x_ref.at[peer, j],
            dst_ref=xbuf.at[j, me],
            send_sem=xsend.at[j, t],
            recv_sem=xrecv.at[j, t],
            device_id={"work": peer},
            device_id_type=MESH,
        )

    own = [
        pltpu.make_async_copy(x_ref.at[me, j], xbuf.at[j, me], own_sem.at[j])
        for j in range(own_a)
    ]
    own.append(pltpu.make_async_copy(legs_ref.at[me], lbuf.at[me], own_sem.at[own_a]))
    for copy in own:
        copy.start()

    barrier = pltpu.get_barrier_semaphore()

    @pl.loop(1, workers)
    def _(t):
        peer = lax.rem(me + t, workers)
        pl.semaphore_signal(barrier, inc=1, device_id={"work": peer}, device_id_type=MESH)

    pl.semaphore_wait(barrier, workers - 1)

    @pl.loop(1, workers)
    def _(t):
        leg_copy(t).start()

    @pl.loop(0, own_a)
    def _(j):
        @pl.loop(1, workers)
        def _(t):
            x_copy(j, t).start()

    start = lax.fori_loop(
        0, workers, lambda s, v: v + jnp.where(s < me, counts_ref[s], 0), jnp.int32(0)
    )
    factors = []
    for d in range(MOST):
        value = weights_ref[jnp.minimum(start + d, diagrams - 1)]
        factors.append(jnp.where(d < counts_ref[me], value, 0.0))

    own[own_a].wait()

    @pl.loop(1, workers)
    def _(t):
        leg_copy(t).wait()

    own_rows = lbuf.shape[2]

    @pl.loop(0, MOST * LEGS)
    def _(m):
        for v in range(workers):
            legs[m, v * own_rows : (v + 1) * own_rows, :] = lbuf[v, m].astype(jnp.float32)

    firsts = []
    for d in range(MOST):
        firsts.append(legs[LEGS * d].astype(jnp.bfloat16))
        p2s[d * extent : (d + 1) * extent, :] = legs[LEGS * d + 1].astype(jnp.bfloat16)
        p3s[d] = legs[LEGS * d + 2].T.astype(jnp.bfloat16)
    side = jnp.concatenate(firsts, axis=1)
    low = 0
    for c, size in enumerate(sizes):
        width = MOST * size * workers
        rows = lax.broadcasted_iota(jnp.int32, (MOST * extent, width), 0)
        chosen = jnp.where(rows == key_ref[c, :, :width], 1.0, 0.0).astype(jnp.bfloat16)
        p1s[c, :, :width] = jnp.dot(side, chosen, preferred_element_type=jnp.float32).astype(
            jnp.bfloat16
        )

    group = 4
    wide = 8
    for c, size in enumerate(sizes):
        count = size * workers
        for j in range(low, low + size):
            own[j].wait()

            @pl.loop(1, workers)
            def _(t):
                x_copy(j, t).wait()

        @pl.loop(0, count // group, unroll=2)
        def _(g):
            j = low + lax.div(g * group, workers)
            v = lax.rem(g * group, workers)
            both = jnp.concatenate([xbuf[j, v + i] for i in range(group)], axis=1)
            for d in range(MOST):
                z = jnp.dot(
                    p2s[d * extent : (d + 1) * extent, :], both, preferred_element_type=jnp.float32
                ).astype(jnp.bfloat16)
                stacked = jnp.concatenate(
                    [z[:, i * extent : (i + 1) * extent] for i in range(group)], axis=0
                )
                y = jnp.dot(stacked, p3s[d], preferred_element_type=jnp.float32) * factors[d]
                for i in range(group):
                    at = pl.multiple_of((d * count + group * g + i) * step, 8)
                    mid[pl.ds(at, extent), :] = y[i * extent : (i + 1) * extent]

        low += size

        def pieces(b):
            cols = [
                mid[pl.ds(wide * b + h, MOST * count, stride=step), :].astype(jnp.bfloat16)
                for h in range(wide)
            ]
            t = jnp.dot(
                p1s[c, :, : MOST * count],
                jnp.concatenate(cols, axis=1),
                preferred_element_type=jnp.float32,
            )
            out = []
            for h in range(wide):
                at = pl.ds(pl.multiple_of((wide * b + h) * extent, 8), extent)
                piece = t[:, h * extent : (h + 1) * extent]
                out.append((at, piece if c == 0 else piece + acc[at, :]))
            return out

        if c < len(sizes) - 1:

            @pl.loop(0, extent // wide)
            def _(b):
                for at, piece in pieces(b):
                    acc[at, :] = piece

        else:

            @pl.loop(0, extent // (2 * wide))
            def _(b):
                for half in range(2):
                    for h, (at, piece) in enumerate(pieces(2 * b + half)):
                        stage[:, half * wide + h, :] = piece
                at = pl.ds(pl.multiple_of(2 * wide * b, 2 * wide), 2 * wide)
                obuf[:, at, :] = stage[:, : 2 * wide, :].astype(jnp.bfloat16)
                pltpu.make_async_copy(obuf.at[:, at], o_ref.at[:, at], out_sem.at[b]).start()

            @pl.loop(0, extent // (2 * wide))
            def _(b):
                at = pl.ds(pl.multiple_of(2 * wide * b, 2 * wide), 2 * wide)
                pltpu.make_async_copy(obuf.at[:, at], o_ref.at[:, at], out_sem.at[b]).wait()


def contract(x, legs, counts, weights, workers):
    own_a, extent = x.shape[1], x.shape[2]
    sizes = split_rows(own_a)
    most = max(sizes) * workers
    keys = np.full((len(sizes), 1, MOST * most), -1)
    low = 0
    for c, size in enumerate(sizes):
        count = size * workers
        col = np.arange(MOST * count)
        at = col % count
        keys[c, 0, : MOST * count] = (
            col // count * extent + at % workers * own_a + low + at // workers
        )
        low += size
    step = extent + PAD
    smem = pl.BlockSpec(memory_space=pltpu.SMEM)
    return pl.pallas_call(
        functools.partial(contract_kernel, workers),
        out_shape=jax.ShapeDtypeStruct((extent, extent, extent), jnp.bfloat16),
        in_specs=[
            smem,
            smem,
            pl.BlockSpec(memory_space=pltpu.VMEM),
            pl.BlockSpec(memory_space=pl.ANY),
            pl.BlockSpec(memory_space=pl.ANY),
        ],
        out_specs=pl.BlockSpec(memory_space=pl.ANY),
        scratch_shapes=[
            pltpu.VMEM((own_a, workers, extent, extent), jnp.bfloat16),
            pltpu.VMEM((workers,) + legs.shape[1:], jnp.bfloat16),
            pltpu.VMEM((MOST * LEGS, extent, extent), jnp.float32),
            pltpu.VMEM((len(sizes), extent, MOST * most), jnp.bfloat16),
            pltpu.VMEM((MOST * extent, extent), jnp.bfloat16),
            pltpu.VMEM((MOST, extent, extent), jnp.bfloat16),
            pltpu.VMEM((MOST * most * step, extent), jnp.float32),
            pltpu.VMEM((extent * extent, extent), jnp.float32),
            pltpu.VMEM((extent, 24, extent), jnp.float32),
            pltpu.VMEM((extent, extent, extent), jnp.bfloat16),
            pltpu.SemaphoreType.DMA((own_a + 1,)),
            pltpu.SemaphoreType.DMA((own_a, workers)),
            pltpu.SemaphoreType.DMA((own_a, workers)),
            pltpu.SemaphoreType.DMA((workers,)),
            pltpu.SemaphoreType.DMA((workers,)),
            pltpu.SemaphoreType.DMA((extent // 16,)),
        ],
        compiler_params=pltpu.CompilerParams(
            vmem_limit_bytes=62 * 1024 * 1024, collective_id=0, has_side_effects=True
        ),
        name="contract",
    )(counts, weights, jnp.asarray(keys, jnp.int32), x, legs)


def per_device(sources, perambs, source_ids, peramb_ids, sink_counts, weights):
    workers = lax.axis_size("work")
    extent = sources.shape[2]
    own_a = sources.shape[1] // extent
    picked, legs = pick(
        sources.reshape(-1, own_a, extent, extent),
        perambs,
        source_ids,
        peramb_ids.reshape(-1),
        sink_counts,
    )
    total = contract(picked, legs, sink_counts, weights, workers)
    return total.reshape(1, extent * extent, extent)


def solution(mesh):
    return jax.shard_map(
        per_device,
        mesh=mesh,
        in_specs=(P("cfg", "work", None), P("cfg", "work"), P(), P(), P(), P()),
        out_specs=P(("cfg", "work"), None, None),
        check_vma=False,
    )
```

```python
import functools

import jax
import jax.numpy as jnp
import numpy as np
from jax import lax
from jax.experimental import pallas as pl
from jax.experimental.pallas import tpu as pltpu
from jax.sharding import PartitionSpec as P

MOST = 6
LEGS = 3
PAD = 8
MESH = pl.DeviceIdType.MESH


def pick_kernel(
    ids_ref, legs_ids_ref, counts_ref, x_ref, p_ref, o_ref, l_ref, rows, sem
):
    sinks = o_ref.shape[0]
    diagrams = legs_ids_ref.shape[1]
    own_rows, extent = l_ref.shape[2], l_ref.shape[3]

    @pl.loop(0, sinks)
    def _(s):
        pltpu.make_async_copy(x_ref.at[ids_ref[s]], o_ref.at[s], sem.at[s]).start()

    for r in range(own_rows):
        rows[:, r, :] = p_ref[:, r * extent : (r + 1) * extent].astype(jnp.float32)

    def one(s, start):
        for slot in range(MOST):
            d = jnp.minimum(start + slot, diagrams - 1)
            for leg in range(LEGS):
                l_ref[s, slot * LEGS + leg] = rows[legs_ids_ref[leg, d]].astype(
                    jnp.bfloat16
                )
        return start + counts_ref[s]

    lax.fori_loop(0, sinks, one, jnp.int32(0))

    @pl.loop(0, sinks)
    def _(s):
        pltpu.make_async_copy(x_ref.at[0], o_ref.at[s], sem.at[s]).wait()


def pick(sources, perambs, source_ids, leg_ids, counts):
    sinks = source_ids.shape[0]
    own_rows, extent = sources.shape[1], sources.shape[3]
    smem = pl.BlockSpec(memory_space=pltpu.SMEM)
    return pl.pallas_call(
        pick_kernel,
        out_shape=(
            jax.ShapeDtypeStruct((sinks,) + sources.shape[1:], sources.dtype),
            jax.ShapeDtypeStruct((sinks, MOST * LEGS, own_rows, extent), perambs.dtype),
        ),
        in_specs=[
            smem,
            smem,
            smem,
            pl.BlockSpec(memory_space=pl.ANY),
            pl.BlockSpec(memory_space=pltpu.VMEM),
        ],
        out_specs=(
            pl.BlockSpec(memory_space=pltpu.VMEM),
            pl.BlockSpec(memory_space=pltpu.VMEM),
        ),
        scratch_shapes=[
            pltpu.VMEM((perambs.shape[0], own_rows, extent), jnp.float32),
            pltpu.SemaphoreType.DMA((sinks,)),
        ],
        compiler_params=pltpu.CompilerParams(vmem_limit_bytes=12 * 1024 * 1024),
        name="pick",
    )(source_ids, leg_ids, counts, sources, perambs)


def split_rows(own_a):
    sizes, left = [], own_a
    while left > 0:
        sizes.append(2 if left > 2 else 1)
        left -= sizes[-1]
    return sizes


def contract_kernel(
    workers,
    counts_ref,
    weights_ref,
    key_ref,
    x_ref,
    legs_ref,
    o_ref,
    xbuf,
    lbuf,
    legs,
    p1s,
    p2s,
    p3s,
    mid,
    acc,
    stage,
    own_sem,
    xsend,
    xrecv,
    lsend,
    lrecv,
):
    own_a, extent = xbuf.shape[0], xbuf.shape[2]
    diagrams = weights_ref.shape[0]
    sizes = split_rows(own_a)
    step = extent + PAD
    me = lax.axis_index("work")

    def leg_copy(t):
        peer = lax.rem(me + t, workers)
        return pltpu.make_async_remote_copy(
            src_ref=legs_ref.at[peer],
            dst_ref=lbuf.at[me],
            send_sem=lsend.at[t],
            recv_sem=lrecv.at[t],
            device_id={"work": peer},
            device_id_type=MESH,
        )

    def x_copy(j, t):
        peer = lax.rem(me + t, workers)
        return pltpu.make_async_remote_copy(
            src_ref=x_ref.at[peer, j],
            dst_ref=xbuf.at[j, me],
            send_sem=xsend.at[j, t],
            recv_sem=xrecv.at[j, t],
            device_id={"work": peer},
            device_id_type=MESH,
        )

    own = [
        pltpu.make_async_copy(x_ref.at[me, j], xbuf.at[j, me], own_sem.at[j])
        for j in range(own_a)
    ]
    own.append(pltpu.make_async_copy(legs_ref.at[me], lbuf.at[me], own_sem.at[own_a]))
    for copy in own:
        copy.start()

    barrier = pltpu.get_barrier_semaphore()

    @pl.loop(1, workers)
    def _(t):
        peer = lax.rem(me + t, workers)
        pl.semaphore_signal(barrier, inc=1, device_id={"work": peer}, device_id_type=MESH)

    pl.semaphore_wait(barrier, workers - 1)

    @pl.loop(1, workers)
    def _(t):
        leg_copy(t).start()

    @pl.loop(0, own_a)
    def _(j):
        @pl.loop(1, workers)
        def _(t):
            x_copy(j, t).start()

    start = lax.fori_loop(
        0, workers, lambda s, v: v + jnp.where(s < me, counts_ref[s], 0), jnp.int32(0)
    )
    factors = []
    for d in range(MOST):
        value = weights_ref[jnp.minimum(start + d, diagrams - 1)]
        factors.append(jnp.where(d < counts_ref[me], value, 0.0))

    own[own_a].wait()

    @pl.loop(1, workers)
    def _(t):
        leg_copy(t).wait()

    own_rows = lbuf.shape[2]

    @pl.loop(0, MOST * LEGS)
    def _(m):
        for v in range(workers):
            legs[m, v * own_rows : (v + 1) * own_rows, :] = lbuf[v, m].astype(jnp.float32)

    firsts = []
    for d in range(MOST):
        firsts.append(legs[LEGS * d].astype(jnp.bfloat16))
        p2s[d * extent : (d + 1) * extent, :] = legs[LEGS * d + 1].astype(jnp.bfloat16)
        p3s[d] = legs[LEGS * d + 2].T.astype(jnp.bfloat16)
    side = jnp.concatenate(firsts, axis=1)
    low = 0
    for c, size in enumerate(sizes):
        width = MOST * size * workers
        rows = lax.broadcasted_iota(jnp.int32, (MOST * extent, width), 0)
        chosen = jnp.where(rows == key_ref[c, :, :width], 1.0, 0.0).astype(jnp.bfloat16)
        p1s[c, :, :width] = jnp.dot(side, chosen, preferred_element_type=jnp.float32).astype(
            jnp.bfloat16
        )

    group = 4
    wide = 8
    for c, size in enumerate(sizes):
        count = size * workers
        for j in range(low, low + size):
            own[j].wait()

            @pl.loop(1, workers)
            def _(t):
                x_copy(j, t).wait()

        @pl.loop(0, count // group, unroll=2)
        def _(g):
            j = low + lax.div(g * group, workers)
            v = lax.rem(g * group, workers)
            both = jnp.concatenate([xbuf[j, v + i] for i in range(group)], axis=1)
            for d in range(MOST):
                z = jnp.dot(
                    p2s[d * extent : (d + 1) * extent, :], both, preferred_element_type=jnp.float32
                ).astype(jnp.bfloat16)
                stacked = jnp.concatenate(
                    [z[:, i * extent : (i + 1) * extent] for i in range(group)], axis=0
                )
                y = jnp.dot(stacked, p3s[d], preferred_element_type=jnp.float32) * factors[d]
                for i in range(group):
                    at = pl.multiple_of((d * count + group * g + i) * step, 8)
                    mid[pl.ds(at, extent), :] = y[i * extent : (i + 1) * extent]

        low += size

        def pieces(b):
            cols = [
                mid[pl.ds(wide * b + h, MOST * count, stride=step), :].astype(jnp.bfloat16)
                for h in range(wide)
            ]
            t = jnp.dot(
                p1s[c, :, : MOST * count],
                jnp.concatenate(cols, axis=1),
                preferred_element_type=jnp.float32,
            )
            out = []
            for h in range(wide):
                at = pl.ds(pl.multiple_of((wide * b + h) * extent, 8), extent)
                piece = t[:, h * extent : (h + 1) * extent]
                out.append((at, piece if c == 0 else piece + acc[at, :]))
            return out

        if c < len(sizes) - 1:

            @pl.loop(0, extent // wide)
            def _(b):
                for at, piece in pieces(b):
                    acc[at, :] = piece

        else:

            @pl.loop(0, extent // (2 * wide))
            def _(b):
                for half in range(2):
                    for h, (at, piece) in enumerate(pieces(2 * b + half)):
                        stage[:, half * wide + h, :] = piece
                at = pl.ds(pl.multiple_of(2 * wide * b, 2 * wide), 2 * wide)
                o_ref[:, at, :] = stage[:, : 2 * wide, :].astype(jnp.bfloat16)


def contract(x, legs, counts, weights, workers):
    own_a, extent = x.shape[1], x.shape[2]
    sizes = split_rows(own_a)
    most = max(sizes) * workers
    keys = np.full((len(sizes), 1, MOST * most), -1)
    low = 0
    for c, size in enumerate(sizes):
        count = size * workers
        col = np.arange(MOST * count)
        at = col % count
        keys[c, 0, : MOST * count] = (
            col // count * extent + at % workers * own_a + low + at // workers
        )
        low += size
    step = extent + PAD
    smem = pl.BlockSpec(memory_space=pltpu.SMEM)
    return pl.pallas_call(
        functools.partial(contract_kernel, workers),
        out_shape=jax.ShapeDtypeStruct((extent, extent, extent), jnp.bfloat16),
        in_specs=[
            smem,
            smem,
            pl.BlockSpec(memory_space=pltpu.VMEM),
            pl.BlockSpec(memory_space=pl.ANY),
            pl.BlockSpec(memory_space=pl.ANY),
        ],
        out_specs=pl.BlockSpec(memory_space=pltpu.VMEM),
        scratch_shapes=[
            pltpu.VMEM((own_a, workers, extent, extent), jnp.bfloat16),
            pltpu.VMEM((workers,) + legs.shape[1:], jnp.bfloat16),
            pltpu.VMEM((MOST * LEGS, extent, extent), jnp.float32),
            pltpu.VMEM((len(sizes), extent, MOST * most), jnp.bfloat16),
            pltpu.VMEM((MOST * extent, extent), jnp.bfloat16),
            pltpu.VMEM((MOST, extent, extent), jnp.bfloat16),
            pltpu.VMEM((MOST * most * step, extent), jnp.float32),
            pltpu.VMEM((extent * extent, extent), jnp.float32),
            pltpu.VMEM((extent, 24, extent), jnp.float32),
            pltpu.SemaphoreType.DMA((own_a + 1,)),
            pltpu.SemaphoreType.DMA((own_a, workers)),
            pltpu.SemaphoreType.DMA((own_a, workers)),
            pltpu.SemaphoreType.DMA((workers,)),
            pltpu.SemaphoreType.DMA((workers,)),
        ],
        compiler_params=pltpu.CompilerParams(
            vmem_limit_bytes=MOST * most * step * extent * 4 + 26 * 1024 * 1024, collective_id=0, has_side_effects=True
        ),
        name="contract",
    )(counts, weights, jnp.asarray(keys, jnp.int32), x, legs)


def per_device(sources, perambs, source_ids, peramb_ids, sink_counts, weights):
    workers = lax.axis_size("work")
    extent = sources.shape[2]
    own_a = sources.shape[1] // extent
    picked, legs = pick(
        sources.reshape(-1, own_a, extent, extent),
        perambs,
        source_ids,
        peramb_ids.T,
        sink_counts,
    )
    total = contract(picked, legs, sink_counts, weights, workers)
    return total.reshape(1, extent * extent, extent)


def solution(mesh):
    return jax.shard_map(
        per_device,
        mesh=mesh,
        in_specs=(P("cfg", "work", None), P("cfg", "work"), P(), P(), P(), P()),
        out_specs=P(("cfg", "work"), None, None),
        check_vma=False,
    )
```
